32 devices in a mesh: ep: 8 (over z, x), tp: 4 (over y, core).
Axes of the slice: x: 2, y: 2, z: 4, core: 2. Of those that a mesh axis runs over, the one named last changes fastest.
Arguments:
- hidden_in: bfloat16 [2048, 3584], P('ep', 'tp'), may hold values from -6 to 6
- moe_gain: bfloat16 [3584], replicated, may hold values from 0.099609375 to 1.8984375
- router_weight: bfloat16 [3584, 256], P('tp'), may hold values from -0.09375 to 0.09375
- expert_ids: int32 [2048, 8], P('ep'), may hold values from 0 to 255, all different within a row; in each aligned block of 256 rows (0 to 255, 256 to 511, ...) at most 16 rows name the same one
- shared_gate: bfloat16 [3584, 1024], P(None, 'tp'), may hold values from -0.09375 to 0.09375
- shared_up: bfloat16 [3584, 1024], P(None, 'tp'), may hold values from -0.09375 to 0.09375
- shared_down: bfloat16 [1024, 3584], P('tp'), may hold values from -0.1875 to 0.1875
- expert_gate: bfloat16 [8, 3584, 1024], P('ep', None, 'tp'), may hold values from -0.09375 to 0.09375
- expert_up: bfloat16 [8, 3584, 1024], P('ep', None, 'tp'), may hold values from -0.09375 to 0.09375
- expert_down: bfloat16 [8, 1024, 3584], P('ep', 'tp'), may hold values from -0.1875 to 0.1875
- attn_gain: bfloat16 [3584], P('tp'), may hold values from 0.099609375 to 1.8984375
- kv_down: bfloat16 [3584, 576], P('tp'), may hold values from -0.09375 to 0.09375
- kv_gain: bfloat16 [512], replicated, may hold values from 0.099609375 to 1.8984375
- doc_lengths: int32 [8, 4], P('ep'), may hold values from 1 to 128, 256 in all within a row
- page_table: int32 [8, 4], P('ep'), may hold values from 0 to 3, each once within a row
Outputs:
- layer_out: bfloat16 [2048, 3584], P('ep', 'tp')
- kv_pages: bfloat16 [8, 4, 64, 576], P('ep', 'tp')
The draws below stay inside these ranges and needn't reach their ends.
Inputs may be any that keep to these rules, and one draw needn't show every extreme that they name: `expert_ids`: each row names 8 different experts. Among the rows of one ep index no expert is named more than 16 times. `doc_lengths`: each row sums to 256. `page_table`: each row holds every number below 4 once.
All inputs are finite; a program needn't handle non-finite values.
Results may differ from the reference program's by a relative error of at most 0.0065.
Values may be sent and summed in bfloat16 or wider, within the bound.
No kernel may reach another device: no remote copies, remote signals or barrier semaphores. Data moves between devices by JAX's collectives and lax.ppermute only.
A program may use at most 128 MiB of HBM per device.

```python
import math
import jax
import jax.numpy as jnp
import numpy as np
from jax import lax

D = 3584
HID = 1024
SHARED = 1024
ROUTED = 256
TOP = 8
CAP = 16
KVR = 512
PAGE = 64
NDOC = 4
TOK_DEV = 256
LAT = 576
EXPERTS = 8
TOKENS = 2048
BLK = 4
N_EP = 8


def levels(key, extent, cuts, low, high):
    def one(axis_at, blocks):
        draws = jax.random.uniform(jax.random.fold_in(jax.random.fold_in(key, 6), axis_at), (blocks,), jnp.float32, low / len(cuts), high / len(cuts))
        return jnp.repeat(jnp.exp(draws), extent[axis_at] // blocks).reshape((-1,) + (1,) * (len(extent) - axis_at - 1))

    loudness = one(*cuts[0])
    for cut in cuts[1:]:
        loudness = loudness * one(*cut)
    return loudness


def split_up(amount, total, reach, lean):
    portions = [(1 << 20) // math.isqrt(rank ** lean) + 1 for rank in range(2, amount + 1)]
    surplus, counts = total - reach - (amount - 1), [1] * (amount - 1)
    while surplus > 0:
        free = [i for i in range(amount - 1) if counts[i] < reach]
        mass, left = sum([portions[i] for i in free]), surplus
        for i in free:
            addition = min(reach - counts[i], max(1, left * portions[i] // mass), surplus)
            counts[i] = counts[i] + addition
            surplus = surplus - addition
    return np.array([reach] + counts)


def uneven_parts(own_key, amount, total, most, skew):
    if amount == 2:
        one = jax.random.randint(own_key, (), max(1, total - most), min(most, total - 1) + 1)
        return jnp.stack([one, total - one])
    tallies = jnp.asarray(split_up(amount, total, most, skew), jnp.int32)
    pairs = (amount - 1) // 2
    giver, receiver = tallies[1:1 + 2 * pairs:2], tallies[2:2 + 2 * pairs:2]
    margin = jnp.minimum(giver - 1, most - receiver)
    moved = jax.random.randint(jax.random.fold_in(own_key, 1), (pairs,), 0, 1 << 20) % (margin + 1)
    tallies = tallies.at[1:1 + 2 * pairs:2].set(giver - moved).at[2:2 + 2 * pairs:2].set(receiver + moved)
    return tallies[jax.random.permutation(jax.random.fold_in(own_key, 2), amount)]


def deal_out(stream_key, own, number, rows, number_of, top, most, skew):
    ranking = jax.random.permutation(stream_key, number_of)
    heavy_load, usual = load_shares(number_of, rows * top, most, skew, True), load_shares(number_of, rows * top, most, skew, False)
    places = jnp.arange(number_of)

    def named(sizes, turn):
        used = int((sizes > 0).sum())
        fixed = max(1, used // 4)
        shifted = fixed + (places - fixed + turn * (used - fixed)) % max(1, number_of - fixed)
        return jnp.zeros((number_of,), jnp.int32).at[ranking[jnp.where(places < fixed, places, shifted)]].set(jnp.asarray(sizes, jnp.int32))

    sizes = jnp.where(number % 4 == 0, named(heavy_load, number // 4), named(usual, number - number // 4 - 1))
    mixed = jax.random.permutation(jax.random.fold_in(own, 3), number_of)
    source_of, taker = mixed[0:number_of // 2 * 2:2], mixed[1:number_of // 2 * 2:2]
    slack = jnp.minimum(sizes[source_of] - 1, most - sizes[taker]) // 2
    slack = jnp.where((source_of == ranking[0]) | (taker == ranking[0]) | (sizes[taker] == 0), 0, jnp.maximum(slack, 0))
    shifted = jax.random.randint(jax.random.fold_in(own, 4), (number_of // 2,), 0, 1 << 20) % (slack + 1)
    sizes = sizes.at[source_of].add(-shifted).at[taker].add(shifted)
    labels = jnp.searchsorted(jnp.cumsum(sizes), jnp.arange(rows * top), side="right").astype(jnp.int32)
    grid = labels.reshape(top, rows).T
    grid = grid[jax.random.permutation(jax.random.fold_in(own, 1), rows)]
    turn = jax.random.randint(jax.random.fold_in(own, 2), (rows, 1), 0, top)
    return jnp.take_along_axis(grid, (jnp.arange(top)[None, :] + turn) % top, axis=1)


def load_shares(amount, total, limit, lean, full):
    portions = [(1 << 20) // math.isqrt(grade ** lean) + 1 for grade in range(1, amount + 1)]
    largest = limit if full else min(limit, max(-(-total // amount), total * portions[0] // sum(portions)))
    least = 1 if total - largest >= amount - 1 else 0
    counts, rest = [largest] + [least] * (amount - 1), total - largest - least * (amount - 1)
    while rest > 0:
        free = [i for i in range(1, amount) if counts[i] < largest] or [i for i in range(1, amount) if counts[i] < limit]
        mass, remaining = sum([portions[i] for i in free]), rest
        for i in free:
            more = min(limit - counts[i], max(1, remaining * portions[i] // mass), rest)
            counts[i] = counts[i] + more
            rest = rest - more
    return np.array(counts)


def centred(key, dims, scale, limit, split=(), kind=jnp.bfloat16):
    values = scale * jax.random.normal(key, dims, jnp.float32)
    if split:
        values = values * levels(key, dims, split, -0.22, 0.18)
    return jnp.clip(values, -limit, limit).astype(kind)


def setup_inputs(seed: int = 0) -> dict:
    seeds = jax.random.split(jax.random.key(seed), 16)
    hidden_in = centred(seeds[0], (TOKENS, D), 1.0, 6.0, ((0, 8), (1, 4)))
    moe_gain = jnp.clip(1.0 + 0.18 * jax.random.normal(seeds[1], (D,), jnp.float32), 0.099609375, 1.8984375).astype(jnp.bfloat16)
    router_weight = centred(seeds[2], (D, ROUTED), D ** -0.5, 0.09375, ((0, 4),))
    expert_ids_keys = jax.random.split(jax.random.fold_in(seeds[3], 1), TOKENS // TOK_DEV)
    expert_ids_turns = jax.random.permutation(jax.random.fold_in(seeds[3], 3), TOKENS // TOK_DEV)
    expert_ids = jax.vmap(lambda own, number: deal_out(jax.random.fold_in(seeds[3], 2), own, number, TOK_DEV, ROUTED, TOP, CAP, 2))(expert_ids_keys, expert_ids_turns).reshape((TOKENS, TOP))
    shared_gate = centred(seeds[4], (D, SHARED), D ** -0.5, 0.09375, ((1, 4),))
    shared_up = centred(seeds[5], (D, SHARED), D ** -0.5, 0.09375, ((1, 4),))
    shared_down = centred(seeds[6], (SHARED, D), SHARED ** -0.5, 0.1875, ((0, 4),))
    expert_gate = centred(seeds[7], (EXPERTS, D, HID), D ** -0.5, 0.09375, ((0, 8), (2, 4)))
    expert_up = centred(seeds[8], (EXPERTS, D, HID), D ** -0.5, 0.09375, ((0, 8), (2, 4)))
    expert_down = centred(seeds[9], (EXPERTS, HID, D), HID ** -0.5, 0.1875, ((0, 8), (1, 4)))
    attn_gain = jnp.clip(1.0 + 0.18 * jax.random.normal(seeds[10], (D,), jnp.float32), 0.099609375, 1.8984375).astype(jnp.bfloat16)
    kv_down = centred(seeds[11], (D, LAT), D ** -0.5, 0.09375, ((0, 4),))
    kv_gain = jnp.clip(1.0 + 0.18 * jax.random.normal(seeds[12], (KVR,), jnp.float32), 0.099609375, 1.8984375).astype(jnp.bfloat16)
    doc_lengths = jax.vmap(lambda own: uneven_parts(own, NDOC, TOK_DEV, TOK_DEV // 2, 2))(jax.random.split(seeds[13], N_EP)).reshape((N_EP, NDOC)).astype(jnp.int32)
    page_table = jax.vmap(lambda own: jax.random.permutation(own, BLK))(jax.random.split(seeds[14], N_EP)).reshape((N_EP, BLK)).astype(jnp.int32)
    return {"hidden_in": hidden_in, "moe_gain": moe_gain, "router_weight": router_weight, "expert_ids": expert_ids, "shared_gate": shared_gate, "shared_up": shared_up, "shared_down": shared_down, "expert_gate": expert_gate, "expert_up": expert_up, "expert_down": expert_down, "attn_gain": attn_gain, "kv_down": kv_down, "kv_gain": kv_gain, "doc_lengths": doc_lengths, "page_table": page_table}


EPS = 1e-06
ROUTE_SCALE = 2.5
THETA = 10000.0

def silu(values):
    return values / (1.0 + jnp.exp(-values))

def route_weights(logits, expert_ids):
    scores = 1.0 / (1.0 + jnp.exp(-logits))
    picked = jnp.take_along_axis(scores, expert_ids, axis=1)
    return ROUTE_SCALE * picked / lax.optimization_barrier(jnp.sum(picked, axis=1, keepdims=True))

def slot_table(expert_ids, gate_weights, expert_count, capacity):
    token_count = expert_ids.shape[0]
    columns = jnp.arange(expert_count, dtype=jnp.int32)
    matched = expert_ids[:, :, None] == columns[None, None, :]
    weight_rows = lax.optimization_barrier(jnp.sum(jnp.where(matched, gate_weights[:, :, None], 0.0), axis=1))
    chosen = jnp.any(matched, axis=1).astype(jnp.int32)
    before = (jnp.cumsum(chosen, axis=0) - chosen).astype(jnp.int32)
    target = jnp.where(chosen > 0, columns[None, :] * capacity + before, expert_count * capacity).astype(jnp.int32)
    token_index = jnp.broadcast_to(jnp.arange(token_count, dtype=jnp.int32)[:, None], target.shape)
    slot_token = jnp.full((expert_count * capacity + 1,), token_count, jnp.int32).at[target.reshape(-1)].set(token_index.reshape(-1))
    slot_weight = jnp.zeros((expert_count * capacity + 1,), jnp.float32).at[target.reshape(-1)].set(weight_rows.reshape(-1))
    return (slot_token[:-1], slot_weight[:-1])

def positions_of(lengths, token_count):
    doc_ends = jnp.cumsum(lengths).astype(jnp.int32)
    doc_starts = (doc_ends - lengths).astype(jnp.int32)
    token_index = jnp.arange(token_count, dtype=jnp.int32)
    doc_begin = lax.optimization_barrier(jnp.max(jnp.where(doc_starts[None, :] <= token_index[:, None], doc_starts[None, :], 0), axis=1))
    return (token_index - doc_begin).astype(jnp.float32)

def rotate(rope_part, position):
    half_width = rope_part.shape[1] // 2
    frequency = THETA ** (-jnp.arange(half_width, dtype=jnp.float32) * 2.0 / rope_part.shape[1])
    angles = position[:, None] * frequency[None, :]
    cosine = jnp.cos(angles)
    sine_part = jnp.sin(angles)
    first_half = rope_part[:, :half_width]
    second_half = rope_part[:, half_width:]
    return jnp.concatenate([first_half * cosine - second_half * sine_part, second_half * cosine + first_half * sine_part], axis=1)

def finish(latent, position, kv_gain):
    plain_part = latent[:, :KVR]
    row_scale = lax.rsqrt(lax.optimization_barrier(jnp.mean(plain_part * plain_part, axis=1, keepdims=True)) + EPS)
    normed = plain_part * row_scale * kv_gain.astype(jnp.float32)
    return jnp.concatenate([normed, rotate(latent[:, KVR:], position)], axis=1).astype(jnp.bfloat16)

def reference(hidden_in, moe_gain, router_weight, expert_ids, shared_gate, shared_up, shared_down, expert_gate, expert_up, expert_down, attn_gain, kv_down, kv_gain, doc_lengths, page_table):
    stream = hidden_in.astype(jnp.float32)
    inverse = lax.rsqrt(lax.optimization_barrier(jnp.mean(stream * stream, axis=1, keepdims=True)) + EPS)
    normed = (stream * inverse * moe_gain.astype(jnp.float32)).astype(jnp.bfloat16)
    logits = jnp.dot(normed, router_weight, preferred_element_type=jnp.float32)
    gate_weights = route_weights(logits, expert_ids)
    shared_hidden = (silu(jnp.dot(normed, shared_gate, preferred_element_type=jnp.float32)) * jnp.dot(normed, shared_up, preferred_element_type=jnp.float32)).astype(jnp.bfloat16)
    shared_out = jnp.dot(shared_hidden, shared_down, preferred_element_type=jnp.float32)

    def block_table(block_ids, block_gates):
        return slot_table(block_ids, block_gates, EXPERTS, CAP)
    slot_token, slot_weight = jax.vmap(block_table)(expert_ids.reshape(N_EP, TOK_DEV, TOP), gate_weights.reshape(N_EP, TOK_DEV, TOP))
    offsets = jnp.arange(N_EP, dtype=jnp.int32)[:, None] * TOK_DEV
    global_token = jnp.where(slot_token < TOK_DEV, slot_token + offsets, TOKENS).astype(jnp.int32)
    row_index = global_token.reshape(N_EP, EXPERTS, CAP).transpose(1, 0, 2).reshape(EXPERTS, N_EP * CAP)
    row_weight = slot_weight.reshape(N_EP, EXPERTS, CAP).transpose(1, 0, 2).reshape(EXPERTS, N_EP * CAP)
    padded = jnp.concatenate([normed, jnp.zeros((1, D), jnp.bfloat16)], axis=0)

    def one_expert(expert_index, routed):
        chosen_rows = row_index[expert_index]
        inputs = padded[chosen_rows]
        hidden_rows = (silu(jnp.dot(inputs, expert_gate[expert_index], preferred_element_type=jnp.float32)) * jnp.dot(inputs, expert_up[expert_index], preferred_element_type=jnp.float32)).astype(jnp.bfloat16)
        result = jnp.dot(hidden_rows, expert_down[expert_index], preferred_element_type=jnp.float32)
        return routed.at[chosen_rows].add(result * row_weight[expert_index][:, None])
    routed = lax.fori_loop(0, EXPERTS, one_expert, jnp.zeros((TOKENS + 1, D), jnp.float32))
    layer_out = (stream + shared_out + routed[:TOKENS]).astype(jnp.bfloat16)
    out_values = layer_out.astype(jnp.float32)
    scaled = (out_values * attn_gain.astype(jnp.float32)).astype(jnp.bfloat16)
    row_stat = lax.rsqrt(lax.optimization_barrier(jnp.mean(out_values * out_values, axis=1, keepdims=True)) + EPS)
    latent = jnp.dot(scaled, kv_down, preferred_element_type=jnp.float32) * row_stat

    def block_positions(lengths):
        return positions_of(lengths, TOK_DEV)
    positions = jax.vmap(block_positions)(doc_lengths).reshape(TOKENS)
    cache_rows = finish(latent, positions, kv_gain).reshape(N_EP, BLK, PAGE, LAT)

    def pick_pages(block_cache, block_slots):
        return block_cache[block_slots]
    kv_pages = jax.vmap(pick_pages)(cache_rows, page_table)
    return (layer_out, kv_pages)
```

```python
import functools

import jax
import jax.numpy as jnp
from jax import lax
from jax.experimental import pallas as pl
from jax.experimental.pallas import tpu as pltpu
from jax.sharding import PartitionSpec as P

CAP = 16
KVR = 512
EPS = 1e-06
ROUTE_SCALE = 2.5
THETA = 10000.0
LANES = 128
F32 = jnp.float32
BF16 = jnp.bfloat16
VMEM = pl.BlockSpec(memory_space=pltpu.VMEM)
SMEM = pl.BlockSpec(memory_space=pltpu.SMEM)


def call(body, out_shape, specs, *operands, flops=1_000_000, limit=None):
    shapes = jax.tree.leaves(out_shape)
    moved = sum(a.size * a.dtype.itemsize for a in operands) + sum(
        s.size * s.dtype.itemsize for s in shapes
    )
    return pl.pallas_call(
        body,
        out_shape=out_shape,
        in_specs=specs,
        out_specs=jax.tree.map(lambda _: VMEM, out_shape),
        cost_estimate=pl.CostEstimate(flops=flops, bytes_accessed=moved, transcendentals=0),
        compiler_params=pltpu.CompilerParams(vmem_limit_bytes=limit),
        name=body.func.__name__ if isinstance(body, functools.partial) else body.__name__,
    )(*operands)


def shape(dims, dtype):
    return jax.ShapeDtypeStruct(dims, dtype)


def dot(a, b):
    return jnp.dot(a, b, preferred_element_type=F32)


def iota(dims, axis):
    return lax.broadcasted_iota(jnp.int32, dims, axis)


def block_at(ref, index, width):
    return pl.ds(pl.multiple_of(index * width, LANES), width)


def transposed_ids(ids):
    rows = ids.shape[0]
    eye = (iota((rows, rows), 0) == iota((rows, rows), 1)).astype(BF16)
    return lax.dot_general(
        ids.astype(F32).astype(BF16), eye, (((0,), (0,)), ((), ())), preferred_element_type=F32
    )


def slot_matrix(ids_t, groups):
    top, rows = ids_t.shape
    expert = iota((groups, rows), 0).astype(F32)
    chosen = jnp.zeros((groups, rows), F32)
    for k in range(top):
        chosen = chosen + jnp.where(ids_t[k : k + 1] == expert, 1.0, 0.0)
    earlier = (iota((rows, rows), 0) < iota((rows, rows), 1)).astype(BF16)
    rank = dot(chosen.astype(BF16), earlier)
    rank = jnp.where(chosen > 0.0, rank, -1.0)
    slot = iota((CAP, rows), 0).astype(F32)
    return jnp.concatenate(
        [jnp.where(rank[e : e + 1] == slot, 1.0, 0.0) for e in range(groups)], axis=0
    )


def pick_rows(groups, ids_ref, hidden_ref, rows_ref):
    chosen = slot_matrix(transposed_ids(ids_ref[...]), groups).astype(BF16)
    rows_ref[...] = dot(chosen, hidden_ref[...]).astype(BF16)


def local_scores(ids_ref, hidden_ref, gain_ref, router_ref, out_ref):
    rows, width = hidden_ref.shape
    member = lax.axis_index("tp")
    x = hidden_ref[...].astype(F32)
    gain = gain_ref[:, block_at(gain_ref, member, width)].astype(F32)
    logits = dot((x * gain).astype(BF16), router_ref[...])
    squares = jnp.sum(x * x, axis=1, keepdims=True)
    both = jnp.concatenate([logits, jnp.broadcast_to(squares, (rows, LANES))], axis=1).T
    experts = router_ref.shape[1]
    ids_t = transposed_ids(ids_ref[...])
    top = ids_t.shape[0]
    index = iota((experts, rows), 0).astype(F32)
    picked = [
        jnp.sum(jnp.where(index == ids_t[k : k + 1], both[:experts], 0.0), axis=0, keepdims=True)
        for k in range(top)
    ]
    out_ref[...] = jnp.concatenate(picked + [both[experts : experts + 8]], axis=0)


def gate_matrix(groups, full_width, ids_ref, mine_ref, theirs_ref, out_ref):
    ids_t = transposed_ids(ids_ref[...])
    top, rows = ids_t.shape
    total = mine_ref[...] + theirs_ref[...]
    inverse = lax.rsqrt(total[top : top + 1] * (1.0 / full_width) + EPS)
    score = 1.0 / (1.0 + jnp.exp(-total[:top] * inverse))
    gate = ROUTE_SCALE * score / jnp.sum(score, axis=0, keepdims=True)
    expert = iota((groups, rows), 0).astype(F32)
    by_expert = jnp.zeros((groups, rows), F32)
    for k in range(top):
        by_expert = by_expert + jnp.where(ids_t[k : k + 1] == expert, gate[k : k + 1], 0.0)
    chosen = slot_matrix(ids_t, groups)
    weights = jnp.concatenate(
        [chosen[e * CAP : (e + 1) * CAP] * by_expert[e : e + 1] for e in range(groups)], axis=0
    ).T
    high = weights.astype(BF16)
    low = (weights - high.astype(F32)).astype(BF16)
    out_ref[...] = jnp.concatenate([high, low], axis=1)


def feed_forward(
    a_ref, b_ref, c_ref, d_ref, gain_ref, gate_ref, up_ref, down_ref, keep_ref, send_ref
):
    width = a_ref.shape[1]
    member = lax.axis_index("tp")
    blocks = [(a_ref, member), (b_ref, member ^ 1), (c_ref, member ^ 2), (d_ref, member ^ 3)]
    squares = 0.0
    for ref, _ in blocks:
        x = ref[...].astype(F32)
        squares = squares + jnp.sum(x * x, axis=1, keepdims=True)
    inverse = lax.rsqrt(squares * (1.0 / (width * len(blocks))) + EPS)
    gate = up = 0.0
    for ref, index in blocks:
        at = block_at(gain_ref, index, width)
        normed = (ref[...].astype(F32) * inverse * gain_ref[:, at].astype(F32)).astype(BF16)
        gate = gate + dot(normed, gate_ref[at, :])
        up = up + dot(normed, up_ref[at, :])
    hidden = (gate / (1.0 + jnp.exp(-gate)) * up).astype(BF16)
    for slot, index in ((0, member ^ 1), (1, member ^ 3)):
        at = block_at(down_ref, index, width)
        send_ref[:, slot * width : (slot + 1) * width] = dot(hidden, down_ref[:, at]).astype(BF16)
    for slot, index in ((0, member), (1, member ^ 2)):
        at = block_at(down_ref, index, width)
        keep_ref[:, slot * width : (slot + 1) * width] = dot(hidden, down_ref[:, at])


def split_pair(value):
    high = value.astype(BF16).astype(F32)
    return high, value - high


def with_energy(latent, energy):
    rows, columns = latent.shape
    padded = -(-(columns + 2) // LANES) * LANES
    lane = iota((rows, padded - columns), 1)
    high, low = split_pair(energy)
    tail = jnp.where(lane == 0, high, jnp.where(lane == 1, low, 0.0))
    return jnp.concatenate([latent, tail], axis=1)


def layer_end(
    pages_ref, routed_ref, gates_ref, hidden_ref, mine_ref, theirs_ref, gain_ref, kv_ref,
    out_ref, keep_ref, send_ref, latent_ref,
):
    member = lax.axis_index("tp")
    rows = routed_ref[...]
    routed = dot(gates_ref[...], jnp.concatenate([rows, rows], axis=0))
    branch = (mine_ref[...] + theirs_ref[...].astype(F32)) + routed
    out = (hidden_ref[...].astype(F32) + branch).astype(BF16)
    out_ref[...] = out
    x = out.astype(F32)
    scaled = (x * gain_ref[...].astype(F32)).astype(BF16)
    energy = jnp.sum(x * x, axis=1, keepdims=True)
    latent_ref[...] = with_energy(dot(scaled, kv_ref[...]), energy)
    page = keep_ref.shape[0] // 2
    for slot, owner in ((0, member), (1, member ^ 2)):
        keep_ref[pl.ds(slot * page, page), :] = latent_ref[page_rows(pages_ref, owner, page), :]
    for slot, owner in ((0, member ^ 1), (1, member ^ 3)):
        send_ref[pl.ds(slot * page, page), :] = latent_ref[
            page_rows(pages_ref, owner, page), :
        ].astype(BF16)


def page_rows(pages_ref, owner, page):
    return pl.ds(pl.multiple_of(pages_ref[0, owner] * page, 16), page)


def latent_half(columns, keep_ref, got_ref, mine_ref, send_ref):
    page = mine_ref.shape[0]
    total = keep_ref[...] + got_ref[...].astype(F32)
    mine_ref[...] = total[:page]
    far = total[page:]
    energy = far[:, columns : columns + 1] + far[:, columns + 1 : columns + 2]
    send_ref[...] = with_energy(far[:, :columns], energy).astype(BF16)


def rope_tables(columns, lengths_ref, pages_ref, cos_ref, sin_ref):
    page = cos_ref.shape[0]
    member = lax.axis_index("tp")
    token = pages_ref[0, member] * page + iota((page, LANES), 0)
    begin = jnp.zeros((page, LANES), jnp.int32)
    start = 0
    for piece in range(lengths_ref.shape[1]):
        begin = jnp.maximum(begin, jnp.where(token >= start, start, 0))
        start = start + lengths_ref[0, piece]
    position = (token - begin).astype(F32)
    half = (columns - KVR) // 2
    lane = iota((page, LANES), 1)
    step = jnp.where(lane < half, lane, lane - half).astype(F32)
    frequency = THETA ** (-step * 2.0 / (2 * half))
    angle = position * frequency
    cos_ref[...] = jnp.cos(angle)
    sine = jnp.sin(angle)
    sin_ref[...] = jnp.where(lane < half, -sine, sine)


def finish(columns, full_width, mine_ref, got_ref, gain_ref, cos_ref, sin_ref, out_ref):
    total = mine_ref[...] + got_ref[...].astype(F32)
    energy = total[:, columns : columns + 1] + total[:, columns + 1 : columns + 2]
    latent = total * lax.rsqrt(energy * (1.0 / full_width) + EPS)
    plain = latent[:, :KVR]
    scale = lax.rsqrt(jnp.mean(plain * plain, axis=1, keepdims=True) + EPS)
    out_ref[:, :KVR] = (plain * scale * gain_ref[...].astype(F32)).astype(BF16)
    rope = latent[:, KVR : KVR + LANES]
    half = (columns - KVR) // 2
    lane = iota(rope.shape, 1)
    other = jnp.where(
        lane < half, pltpu.roll(rope, LANES - half, 1), pltpu.roll(rope, half, 1)
    )
    turned = rope * cos_ref[...] + other * sin_ref[...]
    out_ref[:, KVR:] = turned[:, : columns - KVR].astype(BF16)


def per_device(
    hidden_in,
    moe_gain,
    router_weight,
    expert_ids,
    shared_gate,
    shared_up,
    shared_down,
    expert_gate,
    expert_up,
    expert_down,
    attn_gain,
    kv_down,
    kv_gain,
    doc_lengths,
    page_table,
):
    groups = lax.axis_size("ep")
    members = lax.axis_size("tp")
    rows, width = hidden_in.shape
    full_width = width * members
    slots = groups * CAP
    columns = kv_down.shape[1]
    pages = page_table.shape[1]
    page = rows // pages
    if members != 4 or pages != members or router_weight.shape[1] > 256:
        raise ValueError("unsupported sizes")
    padded = -(-(columns + 2) // LANES) * LANES

    def near(x):
        return lax.ppermute(x, "tp", [(i, i ^ 1) for i in range(members)])

    def far(x):
        return lax.ppermute(x, "tp", [(i, i ^ 2) for i in range(members)])

    def across(x):
        blocks = x.reshape(groups, CAP, width)
        return lax.all_to_all(blocks, "ep", 0, 0, tiled=True).reshape(slots, width)

    gain = moe_gain.reshape(1, full_width)
    far_hidden = far(hidden_in)
    near_hidden = near(hidden_in)
    picked = call(
        functools.partial(pick_rows, groups),
        shape((slots, width), BF16),
        [VMEM] * 2,
        expert_ids,
        hidden_in,
    )
    arrived = across(picked)
    far_rows = far(arrived)
    near_rows = near(arrived)
    diagonal_hidden = near(far_hidden)

    scores = call(
        local_scores,
        shape((16, rows), F32),
        [VMEM] * 4,
        expert_ids,
        hidden_in,
        gain,
        router_weight,
    )
    scores = scores + near(scores)
    far_scores = far(scores)

    def whole_rows(name, a, b, c, d, w_gate, w_up, w_down):
        count = a.shape[0]
        return call(
            feed_forward,
            (shape((count, 2 * width), F32), shape((count, 2 * width), BF16)),
            [VMEM] * 8,
            a,
            b,
            c,
            d,
            gain,
            w_gate,
            w_up,
            w_down,
            flops=6 * count * full_width * w_gate.shape[1],
        )

    def halve(keep, send):
        total = keep + near(send).astype(F32)
        return total[:, :width], total[:, width:].astype(BF16)

    shared_keep, shared_send = whole_rows(
        "shared", hidden_in, near_hidden, far_hidden, diagonal_hidden,
        shared_gate, shared_up, shared_down,
    )
    shared_mine, shared_out = halve(shared_keep, shared_send)
    shared_theirs = far(shared_out)

    diagonal_rows = near(far_rows)
    routed_keep, routed_send = whole_rows(
        "routed", arrived, near_rows, far_rows, diagonal_rows,
        expert_gate[0], expert_up[0], expert_down[0],
    )
    routed_mine, routed_out = halve(routed_keep, routed_send)
    returned = across((routed_mine + far(routed_out).astype(F32)).astype(BF16))

    gates = call(
        functools.partial(gate_matrix, groups, full_width),
        shape((rows, 2 * slots), BF16),
        [VMEM] * 3,
        expert_ids,
        scores,
        far_scores,
    )
    cos, sin = call(
        functools.partial(rope_tables, columns),
        (shape((page, LANES), F32), shape((page, LANES), F32)),
        [SMEM] * 2,
        doc_lengths,
        page_table,
    )
    layer_out, latent_keep, latent_send, _ = call(
        layer_end,
        (
            shape((rows, width), BF16),
            shape((2 * page, padded), F32),
            shape((2 * page, padded), BF16),
            shape((rows, padded), F32),
        ),
        [SMEM] + [VMEM] * 7,
        page_table,
        returned,
        gates,
        hidden_in,
        shared_mine,
        shared_theirs,
        attn_gain.reshape(1, width),
        kv_down,
    )
    latent_mine, latent_out = call(
        functools.partial(latent_half, columns),
        (shape((page, padded), F32), shape((page, padded), BF16)),
        [VMEM] * 2,
        latent_keep,
        near(latent_send),
    )
    page_out = call(
        functools.partial(finish, columns, full_width),
        shape((page, columns), BF16),
        [VMEM] * 5,
        latent_mine,
        far(latent_out),
        kv_gain.reshape(1, KVR),
        cos,
        sin,
    )
    return (layer_out, page_out.reshape(1, 1, page, columns))


def solution(mesh):
    placed = (
        P("ep", "tp"),
        P(),
        P("tp", None),
        P("ep", None),
        P(None, "tp"),
        P(None, "tp"),
        P("tp", None),
        P("ep", None, "tp"),
        P("ep", None, "tp"),
        P("ep", "tp", None),
        P("tp"),
        P("tp", None),
        P(),
        P("ep", None),
        P("ep", None),
    )
    return jax.shard_map(
        per_device,
        mesh=mesh,
        in_specs=placed,
        out_specs=(P("ep", "tp"), P("ep", "tp", None, None)),
        check_vma=False,
    )
```

```python
import functools

import jax
import jax.numpy as jnp
from jax import lax
from jax.experimental import pallas as pl
from jax.experimental.pallas import tpu as pltpu
from jax.sharding import PartitionSpec as P

CAP = 16
KVR = 512
EPS = 1e-06
ROUTE_SCALE = 2.5
THETA = 10000.0
LANES = 128
F32 = jnp.float32
BF16 = jnp.bfloat16
VMEM = pl.BlockSpec(memory_space=pltpu.VMEM)
SMEM = pl.BlockSpec(memory_space=pltpu.SMEM)


def call(body, out_shape, specs, *operands, flops=1_000_000, scratch=()):
    shapes = jax.tree.leaves(out_shape)
    moved = sum(a.size * a.dtype.itemsize for a in operands) + sum(
        s.size * s.dtype.itemsize for s in shapes
    )
    limit = min(2 * moved + (4 << 20), 60 << 20)
    return pl.pallas_call(
        body,
        out_shape=out_shape,
        in_specs=specs,
        out_specs=jax.tree.map(lambda _: VMEM, out_shape),
        scratch_shapes=scratch,
        cost_estimate=pl.CostEstimate(flops=flops, bytes_accessed=moved, transcendentals=0),
        compiler_params=pltpu.CompilerParams(vmem_limit_bytes=limit),
    )(*operands)


def shape(dims, dtype):
    return jax.ShapeDtypeStruct(dims, dtype)


def dot(a, b):
    return jnp.dot(a, b, preferred_element_type=F32)


def dot_t(a, b):
    return lax.dot_general(a, b, (((1,), (1,)), ((), ())), preferred_element_type=F32)


def iota(dims, axis):
    return lax.broadcasted_iota(jnp.int32, dims, axis)


def block_at(index, width):
    return pl.ds(pl.multiple_of(index * width, LANES), width)


def slot_matrix(ids_t, groups):
    top, rows = ids_t.shape
    expert = iota((groups, rows), 0).astype(F32)
    chosen = jnp.zeros((groups, rows), F32)
    for k in range(top):
        chosen = chosen + jnp.where(ids_t[k : k + 1] == expert, 1.0, 0.0)
    earlier = (iota((rows, rows), 0) < iota((rows, rows), 1)).astype(BF16)
    rank = dot(chosen.astype(BF16), earlier)
    rank = jnp.where(chosen > 0.0, rank, -1.0)
    slot = iota((CAP, rows), 0).astype(F32)
    return jnp.concatenate(
        [jnp.where(rank[e : e + 1] == slot, 1.0, 0.0) for e in range(groups)], axis=0
    )


def pick_rows(groups, ids_ref, hidden_ref, rows_ref):
    chosen = slot_matrix(ids_ref[...].astype(F32), groups).astype(BF16)
    rows_ref[...] = dot(chosen, hidden_ref[...]).astype(BF16)


def local_scores(ids_ref, hidden_ref, gain_ref, router_ref, out_ref):
    rows, width = hidden_ref.shape
    member = lax.axis_index("tp")
    x = hidden_ref[...].astype(F32)
    gain = gain_ref[:, block_at(member, width)].astype(F32)
    logits = dot((x * gain).astype(BF16), router_ref[...])
    squares = jnp.sum(x * x, axis=1, keepdims=True)
    both = jnp.concatenate([logits, jnp.broadcast_to(squares, (rows, LANES))], axis=1).T
    experts = router_ref.shape[1]
    ids_t = ids_ref[...].astype(F32)
    top = ids_t.shape[0]
    index = iota((experts, rows), 0).astype(F32)
    picked = [
        jnp.sum(jnp.where(index == ids_t[k : k + 1], both[:experts], 0.0), axis=0, keepdims=True)
        for k in range(top)
    ]
    out_ref[...] = jnp.concatenate(picked + [both[experts : experts + 8]], axis=0)


def gate_matrix(groups, full_width, ids_ref, mine_ref, theirs_ref, out_ref):
    ids_t = ids_ref[...].astype(F32)
    top, rows = ids_t.shape
    total = mine_ref[...] + theirs_ref[...]
    inverse = lax.rsqrt(total[top : top + 1] * (1.0 / full_width) + EPS)
    score = 1.0 / (1.0 + jnp.exp(-total[:top] * inverse))
    gate = ROUTE_SCALE * score / jnp.sum(score, axis=0, keepdims=True)
    expert = iota((groups, rows), 0).astype(F32)
    by_expert = jnp.zeros((groups, rows), F32)
    for k in range(top):
        by_expert = by_expert + jnp.where(ids_t[k : k + 1] == expert, gate[k : k + 1], 0.0)
    chosen = slot_matrix(ids_t, groups)
    weights = jnp.concatenate(
        [chosen[e * CAP : (e + 1) * CAP] * by_expert[e : e + 1] for e in range(groups)], axis=0
    ).T
    high = weights.astype(BF16)
    low = (weights - high.astype(F32)).astype(BF16)
    out_ref[...] = jnp.concatenate([high, low], axis=1)


def feed_forward(
    a_ref, b_ref, c_ref, d_ref, gain_ref, gate_ref, up_ref, down_ref,
    mine_ref, far_ref, send_ref,
):
    width = a_ref.shape[1]
    member = lax.axis_index("tp")
    blocks = [(a_ref, member), (b_ref, member ^ 1), (c_ref, member ^ 2), (d_ref, member ^ 3)]
    squares = 0.0
    for ref, _ in blocks:
        x = ref[...].astype(F32)
        squares = squares + jnp.sum(x * x, axis=1, keepdims=True)
    inverse = lax.rsqrt(squares * (1.0 / (width * len(blocks))) + EPS)
    gate = up = 0.0
    for ref, index in blocks:
        at = block_at(index, width)
        normed = (ref[...].astype(F32) * inverse * gain_ref[:, at].astype(F32)).astype(BF16)
        gate = gate + dot(normed, gate_ref[at, :])
        up = up + dot(normed, up_ref[at, :])
    hidden = (gate / (1.0 + jnp.exp(-gate)) * up).astype(BF16)
    for slot, index in ((0, member ^ 1), (1, member ^ 3)):
        at = block_at(index, width)
        send_ref[:, slot * width : (slot + 1) * width] = dot(hidden, down_ref[:, at]).astype(BF16)
    for ref, index in ((far_ref, member ^ 2), (mine_ref, member)):
        ref[...] = dot(hidden, down_ref[:, block_at(index, width)])


def split_pair(value):
    high = value.astype(BF16).astype(F32)
    return high, value - high


def with_energy(latent, energy):
    rows, columns = latent.shape
    padded = -(-(columns + 2) // LANES) * LANES
    lane = iota((rows, padded - columns), 1)
    high, low = split_pair(energy)
    tail = jnp.where(lane == 0, high, jnp.where(lane == 1, low, 0.0))
    return jnp.concatenate([latent, tail], axis=1)


def layer_end(
    pages_ref, routed_ref, gates_ref, base_ref, gain_ref, kv_ref,
    out_ref, keep_ref, send_ref, latent_ref,
):
    member = lax.axis_index("tp")
    rows = routed_ref[...]
    routed = dot(gates_ref[...], jnp.concatenate([rows, rows], axis=0))
    out = (base_ref[...] + routed).astype(BF16)
    out_ref[...] = out
    x = out.astype(F32)
    scaled = (x * gain_ref[...].astype(F32)).astype(BF16)
    energy = jnp.sum(x * x, axis=1, keepdims=True)
    latent_ref[...] = with_energy(dot_t(scaled, kv_ref[...]), energy)
    page = keep_ref.shape[0] // 2
    for slot, owner in ((0, member), (1, member ^ 2)):
        keep_ref[pl.ds(slot * page, page), :] = latent_ref[page_rows(pages_ref, owner, page), :]
    for slot, owner in ((0, member ^ 1), (1, member ^ 3)):
        send_ref[pl.ds(slot * page, page), :] = latent_ref[
            page_rows(pages_ref, owner, page), :
        ].astype(BF16)


def page_rows(pages_ref, owner, page):
    return pl.ds(pl.multiple_of(pages_ref[0, owner] * page, 16), page)


def latent_half(columns, keep_ref, got_ref, mine_ref, send_ref):
    page = mine_ref.shape[0]
    total = keep_ref[...] + got_ref[...].astype(F32)
    mine_ref[...] = total[:page]
    far = total[page:]
    energy = far[:, columns : columns + 1] + far[:, columns + 1 : columns + 2]
    send_ref[...] = with_energy(far[:, :columns], energy).astype(BF16)


def rope_tables(columns, lengths_ref, pages_ref, cos_ref, sin_ref):
    page = cos_ref.shape[0]
    member = lax.axis_index("tp")
    token = pages_ref[0, member] * page + iota((page, LANES), 0)
    begin = jnp.zeros((page, LANES), jnp.int32)
    start = 0
    for piece in range(lengths_ref.shape[1]):
        begin = jnp.maximum(begin, jnp.where(token >= start, start, 0))
        start = start + lengths_ref[0, piece]
    position = (token - begin).astype(F32)
    half = (columns - KVR) // 2
    lane = iota((page, LANES), 1)
    step = jnp.where(lane < half, lane, lane - half).astype(F32)
    frequency = THETA ** (-step * 2.0 / (2 * half))
    angle = position * frequency
    cos_ref[...] = jnp.cos(angle)
    sine = jnp.sin(angle)
    sin_ref[...] = jnp.where(lane < half, -sine, sine)


def finish(columns, full_width, mine_ref, got_ref, gain_ref, cos_ref, sin_ref, out_ref):
    total = mine_ref[...] + got_ref[...].astype(F32)
    energy = total[:, columns : columns + 1] + total[:, columns + 1 : columns + 2]
    latent = total * lax.rsqrt(energy * (1.0 / full_width) + EPS)
    plain = latent[:, :KVR]
    scale = lax.rsqrt(jnp.mean(plain * plain, axis=1, keepdims=True) + EPS)
    out_ref[:, :KVR] = (plain * scale * gain_ref[...].astype(F32)).astype(BF16)
    rope = latent[:, KVR : KVR + LANES]
    half = (columns - KVR) // 2
    lane = iota(rope.shape, 1)
    other = jnp.where(
        lane < half, pltpu.roll(rope, LANES - half, 1), pltpu.roll(rope, half, 1)
    )
    turned = rope * cos_ref[...] + other * sin_ref[...]
    out_ref[:, KVR:] = turned[:, : columns - KVR].astype(BF16)


def layer(
    hidden_in,
    moe_gain,
    router_weight,
    expert_ids,
    shared_gate,
    shared_up,
    shared_down,
    expert_gate,
    expert_up,
    expert_down,
    attn_gain,
    kv_down,
    kv_gain,
    doc_lengths,
    page_table,
):
    groups = lax.axis_size("ep")
    members = lax.axis_size("tp")
    rows, width = hidden_in.shape
    full_width = width * members
    slots = groups * CAP
    columns = kv_down.shape[1]
    pages = page_table.shape[1]
    page = rows // pages
    if members != 4 or pages != members or router_weight.shape[1] > 256:
        raise ValueError("unsupported sizes")
    padded = -(-(columns + 2) // LANES) * LANES

    def near(x):
        return lax.ppermute(x, "tp", [(i, i ^ 1) for i in range(members)])

    def far(x):
        return lax.ppermute(x, "tp", [(i, i ^ 2) for i in range(members)])

    def across(x):
        blocks = x.reshape(groups, CAP, width)
        return lax.all_to_all(blocks, "ep", 0, 0, tiled=True).reshape(slots, width)

    gain = moe_gain.reshape(1, full_width)
    ids_t = expert_ids.T
    far_hidden = far(hidden_in)
    near_hidden = near(hidden_in)
    picked = call(
        functools.partial(pick_rows, groups),
        shape((slots, width), BF16),
        [VMEM] * 2,
        ids_t,
        hidden_in,
    )
    arrived = across(picked)
    far_rows = far(arrived)
    near_rows = near(arrived)
    diagonal_hidden = near(far_hidden)

    scores = call(
        local_scores,
        shape((16, rows), F32),
        [VMEM] * 4,
        ids_t,
        hidden_in,
        gain,
        router_weight,
    )
    scores = scores + near(scores)
    far_scores = far(scores)

    def whole_rows(a, b, c, d, w_gate, w_up, w_down):
        count = a.shape[0]
        return call(
            feed_forward,
            (
                shape((count, width), F32),
                shape((count, width), F32),
                shape((count, 2 * width), BF16),
            ),
            [VMEM] * 8,
            a,
            b,
            c,
            d,
            gain,
            w_gate,
            w_up,
            w_down,
            flops=6 * count * full_width * w_gate.shape[1],
        )

    def half(keep, got):
        return (keep + got[:, width:].astype(F32)).astype(BF16)

    shared_mine, shared_far, shared_send = whole_rows(
        hidden_in, near_hidden, far_hidden, diagonal_hidden,
        shared_gate, shared_up, shared_down,
    )
    shared_got = near(shared_send)
    shared_out = half(shared_far, shared_got)
    shared_theirs = far(shared_out)
    base = (
        hidden_in.astype(F32)
        + shared_mine
        + shared_got[:, :width].astype(F32)
        + shared_theirs.astype(F32)
    )

    diagonal_rows = near(far_rows)
    routed_mine, routed_far, routed_send = whole_rows(
        arrived, near_rows, far_rows, diagonal_rows,
        expert_gate[0], expert_up[0], expert_down[0],
    )
    routed_got = near(routed_send)
    routed_theirs = far(half(routed_far, routed_got))
    total = routed_mine + routed_got[:, :width].astype(F32) + routed_theirs.astype(F32)
    returned = across(total.astype(BF16))

    gates = call(
        functools.partial(gate_matrix, groups, full_width),
        shape((rows, 2 * slots), BF16),
        [VMEM] * 3,
        ids_t,
        scores,
        far_scores,
    )
    cos, sin = call(
        functools.partial(rope_tables, columns),
        (shape((page, LANES), F32), shape((page, LANES), F32)),
        [SMEM] * 2,
        doc_lengths,
        page_table,
    )
    layer_out, latent_keep, latent_send = call(
        layer_end,
        (
            shape((rows, width), BF16),
            shape((2 * page, padded), F32),
            shape((2 * page, padded), BF16),
        ),
        [SMEM] + [VMEM] * 5,
        page_table,
        returned,
        gates,
        base,
        attn_gain.reshape(1, width),
        kv_down.T,
        scratch=[pltpu.VMEM((rows, padded), F32)],
    )
    latent_mine, latent_out = call(
        functools.partial(latent_half, columns),
        (shape((page, padded), F32), shape((page, padded), BF16)),
        [VMEM] * 2,
        latent_keep,
        near(latent_send),
    )
    page_out = call(
        functools.partial(finish, columns, full_width),
        shape((page, columns), BF16),
        [VMEM] * 5,
        latent_mine,
        far(latent_out),
        kv_gain.reshape(1, KVR),
        cos,
        sin,
    )
    return (layer_out, page_out.reshape(1, 1, page, columns))


def solution(mesh):
    placed = (
        P("ep", "tp"),
        P(),
        P("tp", None),
        P("ep", None),
        P(None, "tp"),
        P(None, "tp"),
        P("tp", None),
        P("ep", None, "tp"),
        P("ep", None, "tp"),
        P("ep", "tp", None),
        P("tp"),
        P("tp", None),
        P(),
        P("ep", None),
        P("ep", None),
    )
    return jax.shard_map(
        layer,
        mesh=mesh,
        in_specs=placed,
        out_specs=(P("ep", "tp"), P("ep", "tp", None, None)),
        check_vma=False,
    )
```
